128 devices in a mesh: group: 4 (over z), shard: 32 (over x, y, core).
Axes of the slice: x: 4, y: 4, z: 4, core: 2. Of those that a mesh axis runs over, the one named last changes fastest.
Arguments:
- vectors: float32 [16384, 256], P(('group', 'shard')), may hold values from -160 to 160
- item_codes: int32 [16384], P(('group', 'shard')), may hold values from 0 to 63, as said below
- coarse_book: float32 [64, 256], replicated, may hold values from -24 to 24
- fine_books: float32 [8, 16384, 256], P('group', 'shard'), may hold values from -2 to 2
Outputs:
- item_grad: float32 [16384, 256], P(('group', 'shard'))
- fine_grad: float32 [8, 16384, 256], P('group', 'shard')
- coarse_grad: float32 [64, 256], replicated
The draws below stay inside these ranges and needn't reach their ends.
Inputs may be any that keep to these rules, and one draw needn't show every extreme that they name: `item_codes`: the items of one device fall into one group at most 32 times, and one group receives exactly 32 items from every device.
All inputs are finite; a program needn't handle non-finite values.
Results may differ from the reference program's by a relative error of at most 0.0003.
Values sent between devices are 32-bit elements; how exact they have to be, the bound alone decides.
No kernel may reach another device: no remote copies, remote signals or barrier semaphores. Data moves between devices by JAX's collectives and lax.ppermute only.
A program may use at most 192 MiB of HBM per device.

```python
import math
import jax
import jax.numpy as jnp
from jax import lax

D = 256
CODEBOOK = 16384
COARSE = 64
ITEM_DEV = 128
GROUPS = 8
SLOT = 32
ITEMS = 16384
N_GROUP = 4
N_SHARD = 32


def layout(key):
    key_star, key_rank, key_score, key_shuffle, key_code = jax.random.split(jax.random.fold_in(key, 7), 5)
    block_count = ITEMS // ITEM_DEV
    per_group = COARSE // GROUPS
    heavy_group = jax.random.randint(key_star, (), 0, GROUPS).astype(jnp.int32)
    ranking = jax.random.permutation(key_rank, GROUPS).astype(jnp.int32)
    others = (heavy_group + 1 + jnp.arange(GROUPS - 1, dtype=jnp.int32)) % GROUPS
    pooled = jnp.repeat(others, SLOT)
    pool_size = (GROUPS - 1) * SLOT
    jitter = jax.random.randint(key_score, (block_count, pool_size), 0, 4096)
    keyed = (jitter + ranking[pooled][None, :] * 256) * 4096 + jnp.arange(pool_size, dtype=jnp.int32)[None, :]
    picked = jnp.argsort(keyed, axis=1)[:, :ITEM_DEV - SLOT]
    chosen = pooled[picked].astype(jnp.int32)
    group_ids = jnp.concatenate([jnp.zeros((block_count, SLOT), jnp.int32) + heavy_group, chosen], 1)
    shuffle_keys = jax.random.randint(key_shuffle, (block_count, ITEM_DEV), 0, 65536) * ITEM_DEV + jnp.arange(ITEM_DEV, dtype=jnp.int32)[None, :]
    shuffle = jnp.argsort(shuffle_keys, axis=1)
    group_ids = jnp.take_along_axis(group_ids, shuffle, 1)
    within = jax.random.randint(key_code, (block_count, ITEM_DEV), 0, per_group)
    return (group_ids * per_group + within).reshape(ITEMS).astype(jnp.int32)


def coarse_draw(key):
    key_normal = jax.random.fold_in(jax.random.fold_in(key, 11), 0)
    standard = jnp.clip(jax.random.normal(key_normal, (COARSE, D), jnp.float32), -6.0, 6.0)
    return standard


def fine_draw(key):
    key_normal = jax.random.fold_in(jax.random.fold_in(key, 13), 0)
    standard = jnp.clip(jax.random.normal(key_normal, (GROUPS, CODEBOOK, D), jnp.float32), -6.0, 6.0)
    return standard / math.sqrt(D)


def draw_item_codes(key, part):
    return layout(key)


def draw_coarse_book(key, part):
    return coarse_draw(key)


def draw_fine_books(key, part):
    return fine_draw(key)


def draw_vectors(key, part):
    item_codes = layout(key)
    offset = coarse_draw(key)[item_codes]
    key_noise = jax.random.fold_in(jax.random.fold_in(key, 17), 0)
    drawn = jnp.clip(jax.random.normal(key_noise, (ITEMS, D), jnp.float32), -6.0, 6.0)
    return offset + drawn


def setup_inputs(seed: int = 0) -> dict:
    key_list = jax.random.split(jax.random.key(seed), 5)
    return {
        "vectors": draw_vectors(jax.random.fold_in(key_list[4], 71), 0),
        "item_codes": draw_item_codes(jax.random.fold_in(key_list[4], 71), 0),
        "coarse_book": draw_coarse_book(jax.random.fold_in(key_list[4], 71), 0),
        "fine_books": draw_fine_books(jax.random.fold_in(key_list[4], 71), 0),
    }


sharpness = 2.5
highest = lax.Precision.HIGHEST


def contract(former, latter, former_dim, latter_dim):
    return lax.dot_general(former, latter, (((former_dim,), (latter_dim,)), ((), ())), precision=highest, preferred_element_type=jnp.float32)


def reference(vectors, item_codes, coarse_book, fine_books):
    groups_all = fine_books.shape[0]
    per_group = COARSE // groups_all
    onehot = (item_codes[:, None] == jnp.arange(COARSE, dtype=jnp.int32)[None, :]).astype(jnp.float32)
    residual = vectors - contract(onehot, coarse_book, 1, 0)
    group_of = (item_codes // per_group).astype(jnp.int32)
    ordering = jnp.argsort(group_of, stable=True).astype(jnp.int32)
    sorted_rows = residual[ordering]
    sorted_group = group_of[ordering]
    counts = jnp.sum((group_of[:, None] == jnp.arange(groups_all, dtype=jnp.int32)[None, :]).astype(jnp.int32), axis=0)
    starts = (jnp.cumsum(counts) - counts).astype(jnp.int32)
    capacity = N_GROUP * N_SHARD * SLOT
    padded = jnp.concatenate([sorted_rows, jnp.zeros((capacity, D), jnp.float32)], 0)

    def one_group(group_index):
        first_row = starts[group_index]
        block_rows = lax.dynamic_slice_in_dim(padded, first_row, capacity, 0)
        live_mask = (jnp.arange(capacity, dtype=jnp.int32) < counts[group_index]).astype(jnp.float32)
        codebook = fine_books[group_index]
        scores = sharpness * contract(block_rows, codebook, 1, 1)
        peak_score = jnp.max(scores, axis=1)
        weights = jnp.exp(scores - peak_score[:, None])
        normalizer = jnp.sum(weights, axis=1)
        quantized = contract(weights, codebook, 1, 0) / normalizer[:, None]
        error_rows = (quantized - block_rows) * live_mask[:, None]
        inner_term = jnp.sum(error_rows * quantized, axis=1)
        probability = weights / normalizer[:, None]
        alignment = contract(error_rows, codebook, 1, 1)
        slopes = probability * (alignment - inner_term[:, None])
        grad_rows = sharpness * contract(slopes, codebook, 1, 0) - error_rows
        book_grad = contract(probability, error_rows, 0, 0) + sharpness * contract(slopes, block_rows, 0, 0)
        return grad_rows, book_grad

    grad_blocks, fine_grad = lax.map(one_group, jnp.arange(groups_all, dtype=jnp.int32))
    slot_of = (jnp.arange(ITEMS, dtype=jnp.int32) - starts[sorted_group]).astype(jnp.int32)
    grad_sorted = grad_blocks[sorted_group, slot_of]
    item_grad = jnp.zeros_like(vectors).at[ordering].set(grad_sorted)
    coarse_grad = -contract(onehot, item_grad, 0, 0)
    return item_grad, fine_grad, coarse_grad
```

```python
import functools

import jax
import jax.numpy as jnp
from jax import lax
from jax.experimental import pallas as pl
from jax.experimental.pallas import tpu as pltpu
from jax.sharding import Mesh, PartitionSpec as P


sharpness = 2.5
F32 = jnp.float32
BF16 = jnp.bfloat16
AXES = ("z", "x", "y", "c")
SLOTS = 32
BLOCK = 40
HOLD = 136
CHUNK = 512


def dot_nn(a, b):
    return lax.dot_general(a, b, (((1,), (0,)), ((), ())), preferred_element_type=F32)


def dot_nt(a, b):
    return lax.dot_general(a, b, (((1,), (1,)), ((), ())), preferred_element_type=F32)


def split2(value):
    high = value.astype(BF16)
    return high, (value - high.astype(F32)).astype(BF16)


def split3(value):
    high = value.astype(BF16)
    rest = value - high.astype(F32)
    middle = rest.astype(BF16)
    return high, middle, (rest - middle.astype(F32)).astype(BF16)


def select_rows(onehot, value):
    chosen = onehot.astype(BF16)
    high, middle, low = split3(value)
    return (dot_nn(chosen, low) + dot_nn(chosen, middle)) + dot_nn(chosen, high)


def to_column(row):
    size = row.shape[1]
    return jnp.transpose(jnp.broadcast_to(row, (size, size)))


def to_row(column):
    size = column.shape[0]
    return jnp.transpose(jnp.broadcast_to(column, (size, size)))[0:1, :]


def iota(shape, dim):
    return lax.broadcasted_iota(jnp.int32, shape, dim)


def targets(code_row, items):
    group_row = code_row // 8
    wide = jnp.broadcast_to(group_row.astype(F32), (items, items))
    same = (jnp.transpose(wide) == wide) & (iota((items, items), 0) < iota((items, items), 1))
    place_row = jnp.sum(same.astype(F32), axis=0, keepdims=True).astype(jnp.int32)
    return group_row, place_row


def route_kernel(z_ref, codes_ref, vectors_ref, coarse_ref, out_ref):
    items, coarse_total = vectors_ref.shape[0], coarse_ref.shape[0]
    code_row = codes_ref[...]
    group_row, place_row = targets(code_row, items)
    code_column = jnp.transpose(jnp.broadcast_to(code_row.astype(F32), (items, items))).astype(jnp.int32)
    onehot = (code_column[:, 0:coarse_total] == iota((items, coarse_total), 1)).astype(F32)
    residual = vectors_ref[...] - select_rows(onehot, coarse_ref[...])
    total = out_ref.shape[0]
    target_row = group_row * BLOCK + place_row
    placing = (iota((total, items), 0) == target_row).astype(F32)
    out_ref[...] = select_rows(placing, residual)
    groups = total // BLOCK
    inner = (code_row - group_row * 8 + 1).astype(F32)
    marks = jnp.where(iota((groups, items), 0) == group_row, inner, 0.0).astype(BF16)
    spots = (iota((items, items), 0) == place_row + SLOTS * z_ref[0]).astype(F32).astype(BF16)
    info = dot_nt(marks, spots)
    for g in range(groups):
        out_ref[g * BLOCK + SLOTS : g * BLOCK + SLOTS + 1, 0:items] = info[g : g + 1, :]


def forward_kernel(rows_ref, *refs):
    blocks = refs[:8]
    high_ref, low_ref, code_high, code_low, part_ref, score_ref, triple_ref = refs[-7:]
    rows = rows_ref[...].reshape(-1, rows_ref.shape[-1])
    count = rows.shape[0]
    high, low = split2(rows)
    triple_ref[...] = jnp.concatenate([high, high, low], axis=1)
    for b in range(8):
        where = slice(b * CHUNK, (b + 1) * CHUNK)
        ch, cl = split2(blocks[b][...].reshape(CHUNK, -1))
        code_high[0, where, :] = ch
        code_low[0, where, :] = cl

    def score_step(b, peak):
        at = pl.ds(pl.multiple_of(b * CHUNK, CHUNK), CHUNK)
        ch = code_high[0, at, :]
        s = dot_nt(triple_ref[...], jnp.concatenate([ch, code_low[0, at, :], ch], axis=1)) * sharpness
        score_ref[:, at] = s
        for t in range(CHUNK // 128):
            peak = jnp.maximum(peak, s[:, t * 128 : (t + 1) * 128])
        return peak

    peak = lax.fori_loop(0, 8, score_step, jnp.full((count, 128), -jnp.inf, F32))
    peak = jnp.max(peak, axis=1, keepdims=True)

    def weight_step(b, carry):
        total, quant = carry
        at = pl.ds(pl.multiple_of(b * CHUNK, CHUNK), CHUNK)
        w = jnp.exp(score_ref[:, at] - peak)
        for t in range(CHUNK // 128):
            total = total + w[:, t * 128 : (t + 1) * 128]
        wh, wl = split2(w)
        high_ref[0, :, at] = wh
        low_ref[0, :, at] = wl
        ch = code_high[0, at, :]
        quant = quant + dot_nn(
            jnp.concatenate([wh, wl, wh], axis=1), jnp.concatenate([ch, ch, code_low[0, at, :]], axis=0)
        )
        return total, quant

    total, quant = lax.fori_loop(
        0, 8, weight_step, (jnp.zeros((count, 128), F32), jnp.zeros((count, rows.shape[1]), F32))
    )
    total = jnp.sum(total, axis=1, keepdims=True)
    held = count // 4
    for y in range(4):
        mine = slice(y * held, (y + 1) * held)
        part_ref[y, 0:held, :] = quant[mine]
        part_ref[y, held : held + 1, 0:held] = to_row(peak[mine])
        part_ref[y, held : held + 1, held : 2 * held] = to_row(total[mine])


def merge_kernel(part_ref, info_ref, out_ref):
    held = 128
    peaks = [to_column(part_ref[y, held : held + 1, 0:held]) for y in range(4)]
    totals = [to_column(part_ref[y, held : held + 1, held : 2 * held]) for y in range(4)]
    peak = functools.reduce(jnp.maximum, peaks)
    scales = [jnp.exp(p - peak) for p in peaks]
    total = functools.reduce(jnp.add, [t * s for t, s in zip(totals, scales)])
    code_row = functools.reduce(jnp.add, [info_ref[z, 0, SLOTS : SLOTS + 1, 0:held] for z in range(4)])
    live = to_column(code_row)[:, 0:1] > 0.5
    quant = functools.reduce(jnp.add, [part_ref[y, 0:held, :] * scales[y][:, 0:1] for y in range(4)])
    quant = jnp.where(live, quant / total[:, 0:1], 0.0)
    for y in range(4):
        out_ref[y, 0:held, :] = quant
        out_ref[y, held : held + 1, 0:held] = to_row(peak[:, 0:1])
        out_ref[y, held : held + 1, held : 2 * held] = to_row(total[:, 0:1])
        out_ref[y, held + 1 : held + 2, 0:held] = code_row


def backward_kernel(y_ref, rows_ref, part_ref, merged_ref, high_ref, low_ref, code_high, code_low, *refs):
    slope_high, slope_low, pushed_ref, coarse_ref, turned_ref, triple_ref = refs[-6:]
    rows = rows_ref[...].reshape(-1, rows_ref.shape[-1])
    count, width = rows.shape
    held = count // 4
    factors = []
    for y in range(4):
        own_peak = to_column(part_ref[y, held : held + 1, 0:held])[:, 0:1]
        peak = to_column(merged_ref[y, held : held + 1, 0:held])[:, 0:1]
        total = to_column(merged_ref[y, held : held + 1, held : 2 * held])[:, 0:1]
        factors.append(jnp.exp(own_peak - peak) / total)
    factor = jnp.concatenate(factors, axis=0)
    quant = jnp.concatenate([merged_ref[y, 0:held, :] for y in range(4)], axis=0)
    live = jnp.concatenate(
        [to_column(merged_ref[y, held + 1 : held + 2, 0:held])[:, 0:1] for y in range(4)], axis=0
    )
    error = jnp.where(live > 0.5, quant - rows, 0.0)
    inner = jnp.sum(error * quant, axis=1, keepdims=True) * factor
    scaled = error * factor
    high, low = split2(scaled)
    triple_ref[...] = jnp.concatenate([high, high, low], axis=1)
    turned_high, turned_low = split2(jnp.transpose(scaled))
    turned_ref[0, 0] = turned_high
    turned_ref[0, 1] = turned_low
    turned_high, turned_low = split2(jnp.transpose(rows * sharpness))
    turned_ref[0, 2] = turned_high
    turned_ref[0, 3] = turned_low

    def step(b, pushed):
        at = pl.ds(pl.multiple_of(b * CHUNK, CHUNK), CHUNK)
        ch = code_high[0, at, :]
        cl = code_low[0, at, :]
        align = dot_nt(triple_ref[...], jnp.concatenate([ch, cl, ch], axis=1))
        w = high_ref[0, :, at].astype(F32) + low_ref[0, :, at].astype(F32)
        sh, sl = split2(w * (align - inner))
        slope_high[0, :, at] = sh
        slope_low[0, :, at] = sl
        return pushed + dot_nn(jnp.concatenate([sh, sl, sh], axis=1), jnp.concatenate([ch, ch, cl], axis=0))

    pushed = lax.fori_loop(0, 8, step, jnp.zeros((count, width), F32)) * sharpness
    mine = (iota((count, 1), 0) // held) == y_ref[0]
    pushed = pushed - jnp.where(mine, error, 0.0)
    code_row = jnp.concatenate([merged_ref[y, held + 1 : held + 2, 0:held] for y in range(4)], axis=1)
    onehot = (iota((8, count), 0) + 1 == code_row.astype(jnp.int32)).astype(F32)
    coarse_ref[...] = -select_rows(onehot, pushed)
    for y in range(4):
        pushed_ref[y] = pushed[y * held : (y + 1) * held]


def grad_kernel(high_ref, low_ref, slope_high, slope_low, turned_ref, own_ref, other_ref):
    left = jnp.concatenate(
        [turned_ref[0, 0], turned_ref[0, 1], turned_ref[0, 0], turned_ref[0, 2], turned_ref[0, 3], turned_ref[0, 2]],
        axis=1,
    )
    for half, out in ((0, own_ref), (1, other_ref)):
        at = slice(half * CHUNK, (half + 1) * CHUNK)
        wh, sh = high_ref[0, :, at], slope_high[0, :, at]
        right = jnp.concatenate([wh, wh, low_ref[0, :, at], sh, sh, slope_low[0, :, at]], axis=0)
        out[0] = dot_nn(left, right)


def turn_kernel(a_ref, b_ref, c_ref, d_ref, out_ref):
    out_ref[0] = jnp.transpose((a_ref[0] + b_ref[0]) + (c_ref[0] + d_ref[0]))


def home_kernel(codes_ref, slots_ref, out_ref):
    items = out_ref.shape[0]
    group_row, place_row = targets(codes_ref[...], items)
    total = slots_ref.shape[0]
    target = (group_row * SLOTS + place_row).astype(F32)
    placing = jnp.transpose(jnp.broadcast_to(target, (items, items)))
    placing = jnp.concatenate([placing] * (total // items), axis=1).astype(jnp.int32)
    out_ref[...] = select_rows((placing == iota((items, total), 1)).astype(F32), slots_ref[...])


def params(**extra):
    return pltpu.CompilerParams(vmem_limit_bytes=60 << 20, **extra)


def whole(shape, dtype=F32):
    return jax.ShapeDtypeStruct(shape, dtype)


SMEM = pl.BlockSpec(memory_space=pltpu.SMEM)
VMEM = pl.BlockSpec(memory_space=pltpu.VMEM)
ANY = pl.BlockSpec(memory_space=pl.ANY)


def cost(flops, moved, exps=0):
    return pl.CostEstimate(flops=flops, bytes_accessed=moved, transcendentals=exps)


def forward(g, rows, blocks, kept):
    width = rows.shape[-1]
    count, codes = 512, 8 * CHUNK
    aliases = {} if kept is None else {1 + 8 + i: i for i in range(4)}
    extra = () if kept is None else kept
    return pl.pallas_call(
        forward_kernel,
        grid=(1,),
        in_specs=[pl.BlockSpec((4, 4, 1, SLOTS, width), lambda i: (0, 0, g, 0, 0))]
        + [
            pl.BlockSpec((1, CHUNK, width), lambda i, g=g: (g, 0, 0))
            if b.shape[0] > 1
            else pl.BlockSpec((1, CHUNK, width), lambda i: (0, 0, 0))
            for b in blocks
        ]
        + [ANY] * len(extra),
        out_specs=[
            pl.BlockSpec((1, count, codes), lambda i: (g, 0, 0)),
            pl.BlockSpec((1, count, codes), lambda i: (g, 0, 0)),
            pl.BlockSpec((1, codes, width), lambda i: (g, 0, 0)),
            pl.BlockSpec((1, codes, width), lambda i: (g, 0, 0)),
            pl.BlockSpec((4, HOLD, width), lambda i: (0, 0, 0)),
        ],
        out_shape=[
            whole((2, count, codes), BF16),
            whole((2, count, codes), BF16),
            whole((2, codes, width), BF16),
            whole((2, codes, width), BF16),
            whole((4, HOLD, width)),
        ],
        scratch_shapes=[pltpu.VMEM((count, codes), F32), pltpu.VMEM((count, 3 * width), BF16)],
        input_output_aliases=aliases,
        compiler_params=params(),
        cost_estimate=cost(12 * count * codes * width, 16 * count * codes, count * codes),
        name=f"forward{g}",
    )(rows, *blocks, *extra)


def backward(g, y, rows, part, merged, weights, kept):
    width = rows.shape[-1]
    high, low, code_high, code_low = weights
    count, codes = 512, 8 * CHUNK
    extra = () if kept is None else kept
    aliases = {} if kept is None else {8: 0, 9: 1, 10: 4}
    big = pl.BlockSpec((1, count, codes), lambda i: (g, 0, 0))
    book = pl.BlockSpec((1, codes, width), lambda i: (g, 0, 0))
    full = pl.BlockSpec((4, HOLD, width), lambda i: (0, 0, 0))
    return pl.pallas_call(
        backward_kernel,
        grid=(1,),
        in_specs=[SMEM, pl.BlockSpec((4, 4, 1, SLOTS, width), lambda i: (0, 0, g, 0, 0)), full, full]
        + [big, big, book, book]
        + [ANY] * len(extra),
        out_specs=[
            big,
            big,
            pl.BlockSpec((4, count // 4, width), lambda i: (0, 0, 0)),
            pl.BlockSpec((8, width), lambda i: (0, 0)),
            pl.BlockSpec((1, 4, width, count), lambda i: (g, 0, 0, 0)),
        ],
        out_shape=[
            whole((2, count, codes), BF16),
            whole((2, count, codes), BF16),
            whole((4, count // 4, width)),
            whole((8, width)),
            whole((2, 4, width, count), BF16),
        ],
        scratch_shapes=[pltpu.VMEM((count, 3 * width), BF16)],
        input_output_aliases=aliases,
        compiler_params=params(),
        cost_estimate=cost(12 * count * codes * width, 16 * count * codes),
        name=f"backward{g}",
    )(y, rows, part, merged, high, low, code_high, code_low, *extra)


def book_grads(j, weights, slopes, turned):
    high, low = weights[:2]
    slope_high, slope_low = slopes
    count, width = high.shape[1], turned.shape[2]
    cut = pl.BlockSpec((1, count, 2 * CHUNK), lambda g: (g, 0, j))
    out = pl.BlockSpec((1, width, CHUNK), lambda g: (g, 0, 0))
    return pl.pallas_call(
        grad_kernel,
        grid=(2,),
        in_specs=[cut, cut, cut, cut, pl.BlockSpec((1, 4, width, count), lambda g: (g, 0, 0, 0))],
        out_specs=[out, out],
        out_shape=[whole((2, width, CHUNK))] * 2,
        compiler_params=params(),
        cost_estimate=cost(2 * 12 * count * 2 * CHUNK * width, 2 * 8 * count * 2 * CHUNK),
        name=f"grads{j}",
    )(high, low, slope_high, slope_low, turned)


def per_device(vectors, item_codes, coarse_book, fine_books):
    items, width = vectors.shape
    shift = lambda a, axis, by: lax.ppermute(a, axis, [(i, (i + by) % 4) for i in range(4)])
    swap = lambda a: lax.ppermute(a, "c", [(0, 1), (1, 0)])
    code_row = item_codes.reshape(1, items)
    z = lax.axis_index("z").astype(jnp.int32).reshape(1)
    y = lax.axis_index("y").astype(jnp.int32).reshape(1)

    from_left = shift(fine_books, "x", 1)
    from_right = shift(fine_books, "x", -1)
    far0 = shift(from_left[0:1], "x", 1)
    far1 = shift(from_right[1:2], "x", -1)
    books = [fine_books, from_left, None, from_right]
    swapped = [swap(fine_books), swap(from_left), None, swap(from_right)]
    fars = [far0, far1]
    swapped_fars = [swap(far0), swap(far1)]

    outgoing = pl.pallas_call(
        route_kernel,
        in_specs=[SMEM, VMEM, VMEM, VMEM],
        out_specs=VMEM,
        out_shape=whole((8 * BLOCK, width)),
        compiler_params=params(),
        name="route",
    )(z, code_row, vectors, coarse_book)
    arrived = lax.all_to_all(outgoing.reshape(4, 2 * BLOCK, width), "z", 0, 0, tiled=True)
    arrived = arrived.reshape(4, 2, BLOCK, width)
    spread = jnp.broadcast_to(arrived[None, :, :, :SLOTS], (4, 4, 2, SLOTS, width))
    rows = lax.all_to_all(spread, "y", 0, 0, tiled=True)

    weights, parts = None, []
    for g in range(2):
        blocks = []
        for j in range(4):
            blocks += [fars[g], swapped_fars[g]] if j == 2 else [books[j], swapped[j]]
        *weights, part = forward(g, rows, blocks, weights)
        parts.append(part)
    merged = []
    for g in range(2):
        got = lax.all_to_all(parts[g], "y", 0, 0, tiled=True)
        out = pl.pallas_call(
            merge_kernel,
            grid=(1,),
            in_specs=[
                pl.BlockSpec((4, HOLD, width), lambda i: (0, 0, 0)),
                pl.BlockSpec((4, 1, BLOCK, width), lambda i, g=g: (0, g, 0, 0)),
            ],
            out_specs=pl.BlockSpec((4, HOLD, width), lambda i: (0, 0, 0)),
            out_shape=whole((4, HOLD, width)),
            compiler_params=params(),
            name=f"merge{g}",
        )(got, arrived)
        merged.append(lax.all_to_all(out, "y", 0, 0, tiled=True))
    kept, pushed, coarse = None, [], []
    for g in range(2):
        sh, sl, push, part_coarse, turned = backward(g, y, rows, parts[g], merged[g], weights, kept)
        kept = (sh, sl, turned)
        pushed.append(push)
        coarse.append(part_coarse)
    slopes, turned = kept[:2], kept[2]

    coarse = jnp.concatenate(coarse, axis=0)
    coarse = coarse + swap(coarse)
    coarse = coarse + shift(coarse, "x", 2)
    coarse = coarse + shift(coarse, "x", 1)

    own, other = book_grads(2, weights, slopes, turned)
    far = own + swap(other)
    far_right = shift(far[0:1], "x", 1)
    far_left = shift(far[1:2], "x", -1)
    own, other = book_grads(3, weights, slopes, turned)
    right = own + swap(other)
    right = jnp.concatenate([right[0:1] + far_right, right[1:2]], axis=0)
    own, other = book_grads(1, weights, slopes, turned)
    left = own + swap(other)
    left = jnp.concatenate([left[0:1], left[1:2] + far_left], axis=0)
    right = shift(right, "x", 1)
    left = shift(left, "x", -1)
    own, other = book_grads(0, weights, slopes, turned)
    block = pl.BlockSpec((1, width, CHUNK), lambda g: (g, 0, 0))
    fine_grad = pl.pallas_call(
        turn_kernel,
        grid=(2,),
        in_specs=[block] * 4,
        out_specs=pl.BlockSpec((1, CHUNK, width), lambda g: (g, 0, 0)),
        out_shape=whole((2, CHUNK, width)),
        compiler_params=params(),
        name="turn",
    )(own, swap(other), right, left)

    held = items
    push = jnp.concatenate(
        [pushed[0], pushed[1], jnp.broadcast_to(coarse[None], (4,) + coarse.shape)], axis=1
    )
    push = jnp.sum(lax.all_to_all(push, "y", 0, 0, tiled=True), axis=0)
    coarse = push[2 * held :]
    push = push[: 2 * held].reshape(2, 4, SLOTS, width).transpose(1, 0, 2, 3).reshape(4, 2 * SLOTS, width)
    push = jnp.concatenate([push, jnp.broadcast_to(coarse[None], (4,) + coarse.shape)], axis=1)
    home = lax.all_to_all(push, "z", 0, 0, tiled=True)
    coarse_grad = home[:, 2 * SLOTS :].reshape(-1, width)
    item_grad = pl.pallas_call(
        home_kernel,
        in_specs=[VMEM, VMEM],
        out_specs=VMEM,
        out_shape=whole((items, width)),
        compiler_params=params(),
        name="home",
    )(code_row, home[:, : 2 * SLOTS].reshape(8 * SLOTS, width))
    return item_grad, fine_grad, coarse_grad


def solution(mesh):
    grid = Mesh(mesh.devices.reshape(4, 4, 4, 2), AXES)
    plane = ("x", "y", "c")
    return jax.shard_map(
        per_device,
        mesh=grid,
        in_specs=(P(AXES, None), P(AXES), P(), P("z", plane, None)),
        out_specs=(P(AXES, None), P("z", plane, None), P()),
        check_vma=False,
    )
```

```python
import functools

import jax
import jax.numpy as jnp
from jax import lax
from jax.experimental import pallas as pl
from jax.experimental.pallas import tpu as pltpu
from jax.sharding import Mesh, PartitionSpec as P


sharpness = 2.5
LOG2E = 1.4426950408889634
F32 = jnp.float32
BF16 = jnp.bfloat16
AXES = ("z", "x", "y", "c")
SLOTS = 32
BLOCK = 40
HOLD = 136
CHUNK = 512


def dot_nn(a, b):
    return lax.dot_general(a, b, (((1,), (0,)), ((), ())), preferred_element_type=F32)


def dot_nt(a, b):
    return lax.dot_general(a, b, (((1,), (1,)), ((), ())), preferred_element_type=F32)


def split2(value):
    high = value.astype(BF16)
    return high, (value - high.astype(F32)).astype(BF16)


def split3(value):
    high = value.astype(BF16)
    rest = value - high.astype(F32)
    middle = rest.astype(BF16)
    return high, middle, (rest - middle.astype(F32)).astype(BF16)


def select_rows(onehot, value):
    chosen = onehot.astype(BF16)
    high, middle, low = split3(value)
    return (dot_nn(chosen, low) + dot_nn(chosen, middle)) + dot_nn(chosen, high)


def iota(shape, dim):
    return lax.broadcasted_iota(jnp.int32, shape, dim)


def targets(code_row, items):
    group_row = code_row // 8
    wide = jnp.broadcast_to(group_row.astype(F32), (items, items))
    same = (jnp.transpose(wide) == wide) & (iota((items, items), 0) < iota((items, items), 1))
    place_row = jnp.sum(same.astype(F32), axis=0, keepdims=True).astype(jnp.int32)
    return group_row, place_row


def route_kernel(z_ref, codes_ref, vectors_ref, coarse_ref, out_ref):
    items, coarse_total = vectors_ref.shape[0], coarse_ref.shape[0]
    code_row = codes_ref[...]
    group_row, place_row = targets(code_row, items)
    code_column = jnp.transpose(jnp.broadcast_to(code_row.astype(F32), (items, items))).astype(jnp.int32)
    onehot = (code_column[:, 0:coarse_total] == iota((items, coarse_total), 1)).astype(F32)
    residual = vectors_ref[...] - select_rows(onehot, coarse_ref[...])
    total = out_ref.shape[0]
    target_row = group_row * BLOCK + place_row
    placing = (iota((total, items), 0) == target_row).astype(F32)
    out_ref[...] = select_rows(placing, residual)
    groups = total // BLOCK
    inner = (code_row - group_row * 8 + 1).astype(F32)
    marks = jnp.where(iota((groups, items), 0) == group_row, inner, 0.0).astype(BF16)
    spots = (iota((items, items), 0) == place_row + SLOTS * z_ref[0]).astype(F32).astype(BF16)
    info = dot_nt(marks, spots)
    for g in range(groups):
        out_ref[g * BLOCK + SLOTS : g * BLOCK + SLOTS + 1, 0:items] = info[g : g + 1, :]


def fetch(blocks, g, book_ref, sems, b):
    source = blocks[b] if len(blocks[b].shape) == 2 else blocks[b].at[g]
    return pltpu.make_async_copy(source, book_ref.at[b], sems.at[b])


def landed(ref, sems, b):
    pltpu.make_async_copy(ref.at[b], ref.at[b], sems.at[b]).wait()


def forward_kernel(g, rows_ref, *refs):
    blocks = refs[:8]
    high_ref, low_ref, part_ref = refs[8:11]
    (score_ref, triple_ref, book_ref, keep_high, keep_low, wide_high, wide_low) = refs[11:18]
    peak_ref, total_ref, quant_ref, sems, high_sems, low_sems = refs[18:]
    count = score_ref.shape[1]
    for b in range(8):
        fetch(blocks, g, book_ref, sems, b).start()
    rows = rows_ref[:, :, g].reshape(count, -1) * (sharpness * LOG2E)
    high, low = split2(rows)
    triple_ref[...] = jnp.concatenate([high, high, low], axis=1)
    peak_ref[...] = jnp.full(peak_ref.shape, -jnp.inf, F32)
    total_ref[...] = jnp.zeros(total_ref.shape, F32)
    quant_ref[...] = jnp.zeros(quant_ref.shape, F32)

    @pl.loop(0, 8)
    def _(b):
        landed(book_ref, sems, b)
        ch, cl = split2(book_ref[b])
        keep_high[b] = ch
        keep_low[b] = cl
        right = jnp.concatenate([ch, cl, ch], axis=1)
        peak = peak_ref[...]
        for half in range(2):
            s = dot_nt(triple_ref[...], right[half * 256 : (half + 1) * 256])
            score_ref[b, :, half * 256 : (half + 1) * 256] = s
            peak = jnp.maximum(peak, jnp.maximum(s[:, 0:128], s[:, 128:256]))
        peak_ref[...] = peak

    peak_ref[...] = jnp.broadcast_to(jnp.max(peak_ref[...], axis=1, keepdims=True), peak_ref.shape)

    @pl.loop(0, 8)
    def _(b):
        peak = peak_ref[...]
        total = total_ref[...]
        left, right = [], []
        for half in range(2):
            at = slice(half * 256, (half + 1) * 256)
            w = jnp.exp2(score_ref[b, :, at] - jnp.concatenate([peak, peak], axis=1))
            total = total + (w[:, 0:128] + w[:, 128:256])
            wh, wl = split2(w)
            wide_high[b, :, at] = wh
            wide_low[b, :, at] = wl
            left += [wh, wl, wh]
            ch = keep_high[b, at, :]
            right += [ch, ch, keep_low[b, at, :]]
        total_ref[...] = total
        quant_ref[...] += dot_nn(jnp.concatenate(left, axis=1), jnp.concatenate(right, axis=0))
        pltpu.make_async_copy(wide_high.at[b], high_ref.at[b], high_sems.at[b]).start()
        pltpu.make_async_copy(wide_low.at[b], low_ref.at[b], low_sems.at[b]).start()

    held = count // 4
    lane = iota((held, 128), 1)
    total = jnp.sum(total_ref[...], axis=1, keepdims=True)
    mixed = jnp.zeros((held, 128), F32)
    for y in range(4):
        mine = slice(y * held, (y + 1) * held)
        part_ref[y, 0:held, :] = quant_ref[mine]
        mixed = jnp.where(lane == 8 * y, peak_ref[mine], mixed)
        mixed = jnp.where(lane == 8 * y + 1, total[mine], mixed)
    mixed = jnp.transpose(mixed)
    for y in range(4):
        part_ref[y, held:HOLD, 0:held] = mixed[8 * y : 8 * y + 8]
        part_ref[y, held:HOLD, held:] = jnp.zeros((8, part_ref.shape[2] - held), F32)
    for b in range(8):
        pltpu.make_async_copy(wide_high.at[b], high_ref.at[b], high_sems.at[b]).wait()
        pltpu.make_async_copy(wide_low.at[b], low_ref.at[b], low_sems.at[b]).wait()


def columns(tiles):
    size = tiles[0].shape[1]
    stacked = jnp.concatenate(tiles, axis=0)
    rest = size - stacked.shape[0]
    if rest:
        stacked = jnp.concatenate([stacked, jnp.zeros((rest, size), F32)], axis=0)
    return jnp.transpose(stacked)


def merge_kernel(part_ref, info_ref, out_ref):
    held = 128
    code_row = functools.reduce(jnp.add, [info_ref[z, 0, SLOTS : SLOTS + 1, 0:held] for z in range(4)])
    turned = columns([part_ref[y, held:HOLD, 0:held] for y in range(4)] + [jnp.broadcast_to(code_row, (8, held))])
    peaks = [turned[:, 8 * y : 8 * y + 1] for y in range(4)]
    totals = [turned[:, 8 * y + 1 : 8 * y + 2] for y in range(4)]
    peak = functools.reduce(jnp.maximum, peaks)
    scales = [jnp.exp2(p - peak) for p in peaks]
    total = functools.reduce(jnp.add, [t * s for t, s in zip(totals, scales)])
    live = turned[:, 32:33] > 0.5
    quant = functools.reduce(jnp.add, [part_ref[y, 0:held, :] * scales[y] for y in range(4)])
    quant = jnp.where(live, quant / total, 0.0)
    lane = iota((held, held), 1)
    mixed = jnp.where(lane == 0, peak, jnp.where(lane == 1, total, turned[:, 32:33]))
    info = jnp.transpose(mixed)[0:8]
    for y in range(4):
        out_ref[y, 0:held, :] = quant
        out_ref[y, held:HOLD, 0:held] = info
        out_ref[y, held:HOLD, held:] = jnp.zeros((8, out_ref.shape[2] - held), F32)


def backward_kernel(g, first, number, resumed, final, joined, y_ref, rows_ref, part_ref, merged_ref, high_ref, low_ref, *refs):
    blocks = refs[:8]
    refs = refs[8:]
    if resumed:
        before_ref, refs = refs[0], refs[1:]
    if joined:
        (push0_ref, coarse0_ref), refs = refs[:2], refs[2:]
    (own_ref, other_ref), refs = refs[:2], refs[2:]
    if joined:
        pushed_ref, refs = refs[0], refs[1:]
    elif final:
        (pushed_ref, coarse_ref), refs = refs[:2], refs[2:]
    else:
        (sofar_ref,), refs = refs[:1], refs[1:]
    triple_ref, left_ref, inner_ref, error_ref, total_ref, book_ref, wide_high, wide_low, wide_grads = refs[:9]
    sems, high_sems, low_sems, grads_sems = refs[9:]
    count, width = error_ref.shape
    held = count // 4

    def loads(b):
        return (
            fetch(blocks, g, book_ref, sems, b),
            pltpu.make_async_copy(high_ref.at[b], wide_high.at[b], high_sems.at[b]),
            pltpu.make_async_copy(low_ref.at[b], wide_low.at[b], low_sems.at[b]),
        )

    for b in range(first, first + number):
        for load in loads(b):
            load.start()
    turned = columns([ref[y, held:HOLD, 0:held] for y in range(4) for ref in (part_ref, merged_ref)])
    for y in range(4):
        mine = slice(y * held, (y + 1) * held)
        at = 16 * y
        factor = jnp.exp2(turned[:, at : at + 1] - turned[:, at + 8 : at + 9]) / turned[:, at + 9 : at + 10]
        rows = rows_ref[y, :, g].reshape(held, width)
        quant = merged_ref[y, 0:held, :]
        error = jnp.where(turned[:, at + 10 : at + 11] > 0.5, quant - rows, 0.0)
        inner = jnp.sum(error * quant, axis=1, keepdims=True) * factor
        scaled = error * factor
        error_ref[mine] = error
        inner_ref[mine] = jnp.broadcast_to(inner, (held, 128))
        high, low = split2(scaled)
        triple_ref[mine] = jnp.concatenate([high, high, low], axis=1)
        for k, value in enumerate((scaled, rows * sharpness)):
            high, low = split2(jnp.transpose(value))
            for part, piece in enumerate((high, low, high)):
                left_ref[:, (3 * k + part) * count + y * held : (3 * k + part) * count + (y + 1) * held] = piece
    if resumed:
        total_ref[...] = before_ref[...]
    else:
        total_ref[...] = jnp.zeros(total_ref.shape, F32)

    @pl.loop(first, first + number)
    def _(b):
        pair = (b - first) // 2
        landed(book_ref, sems, b)
        landed(wide_high, high_sems, b)
        landed(wide_low, low_sems, b)
        ch, cl = split2(book_ref[b])
        right = jnp.concatenate([ch, cl, ch], axis=1)
        inner = inner_ref[...]
        highs, lows = [], []
        for half in range(2):
            align = dot_nt(triple_ref[...], right[half * 256 : (half + 1) * 256])
            for t in range(2):
                at = slice(half * 256 + t * 128, half * 256 + t * 128 + 128)
                w = wide_high[b, :, at].astype(F32) + wide_low[b, :, at].astype(F32)
                sh, sl = split2(w * (align[:, t * 128 : (t + 1) * 128] - inner))
                highs.append(sh)
                lows.append(sl)
        sh = jnp.concatenate(highs, axis=1)
        sl = jnp.concatenate(lows, axis=1)
        wh, wl = wide_high[b], wide_low[b]
        wide_grads[b] = dot_nn(left_ref[...], jnp.concatenate([wh, wh, wl, sh, sh, sl], axis=0))

        @pl.when(b % 2 == 0)
        def _():
            pltpu.make_async_copy(wide_grads.at[b], own_ref.at[pair], grads_sems.at[b]).start()

        @pl.when(b % 2 == 1)
        def _():
            pltpu.make_async_copy(wide_grads.at[b], other_ref.at[pair], grads_sems.at[b]).start()

        total_ref[...] += dot_nn(jnp.concatenate([sh, sl, sh], axis=1), jnp.concatenate([ch, ch, cl], axis=0))

    if final:
        rest = held if joined else 0
        code_row = jnp.concatenate([merged_ref[y, held + 2 : held + 3, 0:held] for y in range(4)], axis=1)
        onehot = (iota((8, count), 0) + 1 == code_row.astype(jnp.int32)).astype(F32)
        coarse = jnp.zeros((8, width), F32)
        for y in range(4):
            mine = slice(y * held, (y + 1) * held)
            pushed = total_ref[mine] * sharpness - jnp.where(y_ref[0] == y, error_ref[mine], 0.0)
            pushed_ref[y, rest : rest + held] = pushed
            coarse = coarse - select_rows(onehot[:, mine], pushed)
        if joined:
            for y in range(4):
                pushed_ref[y, 0:held] = push0_ref[y]
                pushed_ref[y, 2 * held : 2 * held + 8] = coarse0_ref[...]
                pushed_ref[y, 2 * held + 8 : 2 * held + 16] = coarse
        else:
            coarse_ref[...] = coarse
    else:
        sofar_ref[...] = total_ref[...]
    for b in range(first, first + number):
        out = own_ref if b % 2 == 0 else other_ref
        pltpu.make_async_copy(wide_grads.at[b], out.at[(b - first) // 2], grads_sems.at[b]).wait()


def turn_kernel(own_ref, other_ref, right_ref, left_ref, far_ref, *refs):
    near = (own_ref[0] + other_ref[0]) + (right_ref[...] + left_ref[...])
    refs[-1][0] = jnp.transpose(near + far_ref[...])


def home_kernel(codes_ref, slots_ref, out_ref):
    items, width = out_ref.shape
    group_row, place_row = targets(codes_ref[...], items)
    total = slots_ref.shape[0] * slots_ref.shape[1]
    target = (group_row // 2) * slots_ref.shape[1] + (group_row % 2) * SLOTS + place_row
    target = jnp.transpose(jnp.broadcast_to(target.astype(F32), (items, items)))[:, 0:1].astype(jnp.int32)
    onehot = (target == iota((items, total), 1)).astype(F32)
    out_ref[...] = select_rows(onehot, slots_ref[...].reshape(total, width))


def params(mebibytes=8):
    return pltpu.CompilerParams(vmem_limit_bytes=mebibytes << 20)


def whole(shape, dtype=F32):
    return jax.ShapeDtypeStruct(shape, dtype)


SMEM = pl.BlockSpec(memory_space=pltpu.SMEM)
VMEM = pl.BlockSpec(memory_space=pltpu.VMEM)
ANY = pl.BlockSpec(memory_space=pl.ANY)


def cost(flops, moved, exps=0):
    return pl.CostEstimate(flops=flops, bytes_accessed=moved, transcendentals=exps)


def dmas():
    return pltpu.SemaphoreType.DMA((8,))


def forward(g, rows, blocks):
    width = rows.shape[-1]
    count = 512
    return pl.pallas_call(
        functools.partial(forward_kernel, g),
        in_specs=[VMEM] + [ANY] * 8,
        out_specs=[ANY, ANY, VMEM],
        out_shape=[
            whole((8, count, CHUNK), BF16),
            whole((8, count, CHUNK), BF16),
            whole((4, HOLD, width)),
        ],
        scratch_shapes=[
            pltpu.VMEM((8, count, CHUNK), F32),
            pltpu.VMEM((count, 3 * width), BF16),
            pltpu.VMEM((8, CHUNK, width), F32),
            pltpu.VMEM((8, CHUNK, width), BF16),
            pltpu.VMEM((8, CHUNK, width), BF16),
            pltpu.VMEM((8, count, CHUNK), BF16),
            pltpu.VMEM((8, count, CHUNK), BF16),
            pltpu.VMEM((count, 128), F32),
            pltpu.VMEM((count, 128), F32),
            pltpu.VMEM((count, width), F32),
            dmas(),
            dmas(),
            dmas(),
        ],
        compiler_params=params(60),
        cost_estimate=cost(12 * count * 8 * CHUNK * width, 12 * count * 8 * CHUNK, count * 8 * CHUNK),
    )(rows, *blocks)


def backward(g, first, number, y, rows, part, merged, weights, blocks, before, final, joined=()):
    width = rows.shape[-1]
    count = 512
    resumed = before is not None
    out_shape = [whole((number // 2, width, CHUNK))] * 2
    if joined:
        out_shape += [whole((4, count // 2 + 16, width))]
    elif final:
        out_shape += [whole((4, count // 4, width)), whole((8, width))]
    else:
        out_shape += [whole((count, width))]
    return pl.pallas_call(
        functools.partial(backward_kernel, g, first, number, resumed, final, bool(joined)),
        in_specs=[SMEM, VMEM, VMEM, VMEM] + [ANY] * 10 + [VMEM] * (resumed + len(joined)),
        out_specs=[ANY, ANY] + [VMEM] * (len(out_shape) - 2),
        out_shape=out_shape,
        scratch_shapes=[
            pltpu.VMEM((count, 3 * width), BF16),
            pltpu.VMEM((width, 6 * count), BF16),
            pltpu.VMEM((count, 128), F32),
            pltpu.VMEM((count, width), F32),
            pltpu.VMEM((count, width), F32),
            pltpu.VMEM((8, CHUNK, width), F32),
            pltpu.VMEM((8, count, CHUNK), BF16),
            pltpu.VMEM((8, count, CHUNK), BF16),
            pltpu.VMEM((8, width, CHUNK), F32),
            dmas(),
            dmas(),
            dmas(),
            dmas(),
        ],
        compiler_params=params(60),
        cost_estimate=cost(24 * count * number * CHUNK * width, 8 * count * number * CHUNK),
    )(y, rows, part, merged, *weights, *blocks, *((before,) if resumed else ()), *joined)


def after(value, *others):
    return lax.optimization_barrier((value,) + others)[0]


def step(vectors, item_codes, coarse_book, fine_books):
    items, width = vectors.shape
    shift = lambda a, axis, by: lax.ppermute(a, axis, [(i, (i + by) % 4) for i in range(4)])
    swap = lambda a: lax.ppermute(a, "c", [(0, 1), (1, 0)])
    code_row = item_codes.reshape(1, items)
    z = lax.axis_index("z").astype(jnp.int32).reshape(1)
    y = lax.axis_index("y").astype(jnp.int32).reshape(1)

    def travel(book):
        return [shift(book, "x", by) for by in (1, -1, 2)]

    own = [fine_books[0], fine_books[1]]
    near = [travel(own[0])]
    outgoing = pl.pallas_call(
        route_kernel,
        in_specs=[SMEM, VMEM, VMEM, VMEM],
        out_specs=VMEM,
        out_shape=whole((8 * BLOCK, width)),
        compiler_params=params(),
        name="route",
    )(z, code_row, vectors, coarse_book)
    arrived = lax.all_to_all(outgoing.reshape(4, 2 * BLOCK, width), "z", 0, 0, tiled=True)
    near.append(travel(after(own[1], arrived)))
    arrived = arrived.reshape(4, 2, BLOCK, width)
    spread = jnp.broadcast_to(arrived[None, :, :, :SLOTS], (4, 4, 2, SLOTS, width))
    rows = lax.all_to_all(spread, "y", 0, 0, tiled=True)

    books, weights, parts = [], [], []
    for g in range(2):
        left, right, far = near[g]
        if g:
            left, right, far, own[g], _ = lax.optimization_barrier((left, right, far, own[g], parts[0]))
        blocks = []
        for book in (far, left, right, own[g]):
            blocks += [book, swap(book)]
        *weight, part = forward(g, rows, blocks)
        books.append(blocks)
        weights.append(weight)
        parts.append(part)

    def exchange(g, part):
        got = lax.all_to_all(part, "y", 0, 0, tiled=True)
        out = pl.pallas_call(
            merge_kernel,
            grid=(1,),
            in_specs=[
                pl.BlockSpec((4, HOLD, width), lambda i: (0, 0, 0)),
                pl.BlockSpec((4, 1, BLOCK, width), lambda i: (0, g, 0, 0)),
            ],
            out_specs=pl.BlockSpec((4, HOLD, width), lambda i: (0, 0, 0)),
            out_shape=whole((4, HOLD, width)),
            compiler_params=params(),
        )(got, arrived)
        return lax.all_to_all(out, "y", 0, 0, tiled=True)

    merged = [exchange(0, parts[0])]
    merged.append(exchange(1, after(parts[1], merged[0])))

    def return_books(g, calls, before):
        pieces = []
        for when, (own, other) in enumerate(calls):
            got = swap(other)
            pieces += [(own, got, i, when) for i in range(own.shape[0])]
        got = []
        for (own, other, i, when), by in zip(pieces, (2, -1, 1)):
            total = own[i] + other[i]
            got.append(shift(total, "x", by))
        own, other, i, _ = pieces[3]
        pair = pl.BlockSpec((1, width, CHUNK), lambda k: (i, 0, 0))
        flat = pl.BlockSpec((width, CHUNK), lambda k: (0, 0))
        return pl.pallas_call(
            turn_kernel,
            grid=(1,),
            in_specs=[pair, pair, flat, flat, flat] + [ANY] * len(before),
            out_specs=pl.BlockSpec((1, CHUNK, width), lambda k: (g, 0, 0)),
            out_shape=whole((2, CHUNK, width)),
            input_output_aliases={5: 0} if before else {},
            compiler_params=params(),
        )(own, other, *got, *before)

    def gradients(g, counts, joined, before):
        common = (y, rows, parts[g], merged[g], weights[g], books[g])
        calls, first, sofar = [], 0, None
        for number in counts:
            final = first + number == 8
            own, other, *rest = backward(g, first, number, *common, sofar, final, joined if final else ())
            calls.append((own, other))
            first, sofar = first + number, rest[0]
        return return_books(g, calls, before), rest

    fine, joined = gradients(0, (4, 4), (), ())
    fine, (push,) = gradients(1, (4, 2, 2), tuple(joined), (fine,))

    held = items
    push = lax.all_to_all(push, "y", 0, 0, tiled=True)
    push = jnp.sum(push, axis=0)
    coarse = push[2 * held :]
    push = push[: 2 * held].reshape(2, 4, SLOTS, width).transpose(1, 0, 2, 3).reshape(4, 2 * SLOTS, width)
    push = jnp.concatenate([push, jnp.broadcast_to(coarse[None], (4,) + coarse.shape)], axis=1)
    home = lax.all_to_all(push, "z", 0, 0, tiled=True)
    coarse = home[:, 2 * SLOTS :].reshape(-1, width)
    coarse = coarse + swap(coarse)
    others = [shift(coarse, "x", by) for by in (1, 2, 3)]
    coarse = (coarse + others[1]) + (others[0] + others[2])
    item_grad = pl.pallas_call(
        home_kernel,
        in_specs=[VMEM, VMEM],
        out_specs=VMEM,
        out_shape=whole((items, width)),
        compiler_params=params(),
        name="home",
    )(code_row, home)
    return item_grad, fine, coarse


def solution(mesh):
    grid = Mesh(mesh.devices.reshape(4, 4, 4, 2), AXES)
    plane = ("x", "y", "c")
    return jax.shard_map(
        step,
        mesh=grid,
        in_specs=(P(AXES, None), P(AXES), P(), P("z", plane, None)),
        out_specs=(P(AXES, None), P("z", plane, None), P()),
        check_vma=False,
    )
```

```python
import functools

import jax
import jax.numpy as jnp
from jax import lax
from jax.experimental import pallas as pl
from jax.experimental.pallas import tpu as pltpu
from jax.sharding import Mesh, PartitionSpec as P


sharpness = 2.5
LOG2E = 1.4426950408889634
F32 = jnp.float32
BF16 = jnp.bfloat16
AXES = ("z", "x", "y", "c")
SLOTS = 32
BLOCK = 40
HOLD = 136
CHUNK = 512


def dot_nn(a, b):
    return lax.dot_general(a, b, (((1,), (0,)), ((), ())), preferred_element_type=F32)


def dot_nt(a, b):
    return lax.dot_general(a, b, (((1,), (1,)), ((), ())), preferred_element_type=F32)


def split2(value):
    high = value.astype(BF16)
    return high, (value - high.astype(F32)).astype(BF16)


def split3(value):
    high = value.astype(BF16)
    rest = value - high.astype(F32)
    middle = rest.astype(BF16)
    return high, middle, (rest - middle.astype(F32)).astype(BF16)


def select_rows(onehot, value):
    chosen = onehot.astype(BF16)
    high, middle, low = split3(value)
    return (dot_nn(chosen, low) + dot_nn(chosen, middle)) + dot_nn(chosen, high)


def iota(shape, dim):
    return lax.broadcasted_iota(jnp.int32, shape, dim)


def targets(code_row, items):
    group_row = code_row // 8
    wide = jnp.broadcast_to(group_row.astype(F32), (items, items))
    same = (jnp.transpose(wide) == wide) & (iota((items, items), 0) < iota((items, items), 1))
    place_row = jnp.sum(same.astype(F32), axis=0, keepdims=True).astype(jnp.int32)
    return group_row, place_row


def route_kernel(z_ref, codes_ref, vectors_ref, coarse_ref, out_ref):
    items, coarse_total = vectors_ref.shape[0], coarse_ref.shape[0]
    code_row = codes_ref[...]
    group_row, place_row = targets(code_row, items)
    code_column = jnp.transpose(jnp.broadcast_to(code_row.astype(F32), (items, items))).astype(jnp.int32)
    onehot = (code_column[:, 0:coarse_total] == iota((items, coarse_total), 1)).astype(F32)
    residual = vectors_ref[...] - select_rows(onehot, coarse_ref[...])
    total = out_ref.shape[0]
    target_row = group_row * BLOCK + place_row
    placing = (iota((total, items), 0) == target_row).astype(F32)
    out_ref[...] = select_rows(placing, residual)
    groups = total // BLOCK
    inner = (code_row - group_row * 8 + 1).astype(F32)
    marks = jnp.where(iota((groups, items), 0) == group_row, inner, 0.0).astype(BF16)
    spots = (iota((items, items), 0) == place_row + SLOTS * z_ref[0]).astype(F32).astype(BF16)
    info = dot_nt(marks, spots)
    for g in range(groups):
        out_ref[g * BLOCK + SLOTS : g * BLOCK + SLOTS + 1, 0:items] = info[g : g + 1, :]


def fetch(blocks, g, book_ref, sems, b):
    source = blocks[b] if len(blocks[b].shape) == 2 else blocks[b].at[g]
    return pltpu.make_async_copy(source, book_ref.at[b], sems.at[b])


def landed(ref, sems, b):
    pltpu.make_async_copy(ref.at[b], ref.at[b], sems.at[b]).wait()


def forward_kernel(g, *refs):
    row_refs, blocks = refs[:4], refs[4:12]
    high_ref, low_ref = refs[12:14]
    part_refs = refs[14:18]
    (score_ref, triple_ref, book_ref, keep_high, keep_low, wide_high, wide_low) = refs[18:25]
    peak_ref, total_ref, quant_ref, sems, high_sems, low_sems = refs[25:]
    count = score_ref.shape[1]
    for b in range(8):
        fetch(blocks, g, book_ref, sems, b).start()
    rows = jnp.concatenate([ref[:, g].reshape(count // 4, -1) for ref in row_refs], axis=0) * (sharpness * LOG2E)
    high, low = split2(rows)
    triple_ref[...] = jnp.concatenate([high, high, low], axis=1)
    peak_ref[...] = jnp.full(peak_ref.shape, -jnp.inf, F32)
    total_ref[...] = jnp.zeros(total_ref.shape, F32)
    quant_ref[...] = jnp.zeros(quant_ref.shape, F32)

    @pl.loop(0, 8)
    def _(b):
        landed(book_ref, sems, b)
        ch, cl = split2(book_ref[b])
        keep_high[b] = ch
        keep_low[b] = cl
        right = jnp.concatenate([ch, cl, ch], axis=1)
        peak = peak_ref[...]
        for half in range(2):
            s = dot_nt(triple_ref[...], right[half * 256 : (half + 1) * 256])
            score_ref[b, :, half * 256 : (half + 1) * 256] = s
            peak = jnp.maximum(peak, jnp.maximum(s[:, 0:128], s[:, 128:256]))
        peak_ref[...] = peak

    peak_ref[...] = jnp.broadcast_to(jnp.max(peak_ref[...], axis=1, keepdims=True), peak_ref.shape)

    @pl.loop(0, 8)
    def _(b):
        peak = peak_ref[...]
        total = total_ref[...]
        left, right = [], []
        for half in range(2):
            at = slice(half * 256, (half + 1) * 256)
            w = jnp.exp2(score_ref[b, :, at] - jnp.concatenate([peak, peak], axis=1))
            total = total + (w[:, 0:128] + w[:, 128:256])
            wh, wl = split2(w)
            wide_high[b, :, at] = wh
            wide_low[b, :, at] = wl
            left += [wh, wl, wh]
            ch = keep_high[b, at, :]
            right += [ch, ch, keep_low[b, at, :]]
        total_ref[...] = total
        quant_ref[...] += dot_nn(jnp.concatenate(left, axis=1), jnp.concatenate(right, axis=0))
        pltpu.make_async_copy(wide_high.at[b], high_ref.at[b], high_sems.at[b]).start()
        pltpu.make_async_copy(wide_low.at[b], low_ref.at[b], low_sems.at[b]).start()

    held = count // 4
    lane = iota((held, 128), 1)
    total = jnp.sum(total_ref[...], axis=1, keepdims=True)
    mixed = jnp.zeros((held, 128), F32)
    for y in range(4):
        mine = slice(y * held, (y + 1) * held)
        part_refs[y][0:held, :] = quant_ref[mine]
        mixed = jnp.where(lane == 8 * y, peak_ref[mine], mixed)
        mixed = jnp.where(lane == 8 * y + 1, total[mine], mixed)
    mixed = jnp.transpose(mixed)
    for y in range(4):
        part_refs[y][held:HOLD, 0:held] = mixed[8 * y : 8 * y + 8]
        part_refs[y][held:HOLD, held:] = jnp.zeros((8, part_refs[y].shape[1] - held), F32)
    for b in range(8):
        pltpu.make_async_copy(wide_high.at[b], high_ref.at[b], high_sems.at[b]).wait()
        pltpu.make_async_copy(wide_low.at[b], low_ref.at[b], low_sems.at[b]).wait()


def columns(tiles):
    size = tiles[0].shape[1]
    stacked = jnp.concatenate(tiles, axis=0)
    rest = size - stacked.shape[0]
    if rest:
        stacked = jnp.concatenate([stacked, jnp.zeros((rest, size), F32)], axis=0)
    return jnp.transpose(stacked)


def merge_kernel(part0_ref, part1_ref, part2_ref, part3_ref, info_ref, out_ref):
    parts = (part0_ref, part1_ref, part2_ref, part3_ref)
    held = 128
    code_row = functools.reduce(jnp.add, [info_ref[z, 0, SLOTS : SLOTS + 1, 0:held] for z in range(4)])
    turned = columns([part[held:HOLD, 0:held] for part in parts] + [jnp.broadcast_to(code_row, (8, held))])
    peaks = [turned[:, 8 * y : 8 * y + 1] for y in range(4)]
    totals = [turned[:, 8 * y + 1 : 8 * y + 2] for y in range(4)]
    peak = functools.reduce(jnp.maximum, peaks)
    scales = [jnp.exp2(p - peak) for p in peaks]
    total = functools.reduce(jnp.add, [t * s for t, s in zip(totals, scales)])
    live = turned[:, 32:33] > 0.5
    quant = functools.reduce(jnp.add, [parts[y][0:held, :] * scales[y] for y in range(4)])
    quant = jnp.where(live, quant / total, 0.0)
    lane = iota((held, held), 1)
    mixed = jnp.where(lane == 0, peak, jnp.where(lane == 1, total, turned[:, 32:33]))
    info = jnp.transpose(mixed)[0:8]
    out_ref[0:held, :] = quant
    out_ref[held:HOLD, 0:held] = info
    out_ref[held:HOLD, held:] = jnp.zeros((8, out_ref.shape[1] - held), F32)


def backward_kernel(g, first, number, resumed, final, joined, *refs):
    row_refs, part_refs, merged_refs = refs[:4], refs[4:8], refs[8:12]
    (high_ref, low_ref), blocks, refs = refs[12:14], refs[14:22], refs[22:]
    if resumed:
        before_ref, refs = refs[0], refs[1:]
    if joined:
        push0_refs, coarse0_ref, refs = refs[:4], refs[4], refs[5:]
    (own_ref, other_ref), refs = refs[:2], refs[2:]
    if final:
        pushed_refs, refs = refs[:4], refs[4:]
    if final and not joined:
        coarse_ref, refs = refs[0], refs[1:]
    if not final:
        sofar_ref, refs = refs[0], refs[1:]
    triple_ref, left_ref, inner_ref, error_ref, total_ref, book_ref, wide_high, wide_low, wide_grads = refs[:9]
    sems, high_sems, low_sems, grads_sems = refs[9:]
    count, width = error_ref.shape
    held = count // 4

    def loads(b):
        return (
            fetch(blocks, g, book_ref, sems, b),
            pltpu.make_async_copy(high_ref.at[b], wide_high.at[b], high_sems.at[b]),
            pltpu.make_async_copy(low_ref.at[b], wide_low.at[b], low_sems.at[b]),
        )

    for b in range(first, first + number):
        for load in loads(b):
            load.start()
    turned = columns([ref[held:HOLD, 0:held] for pair in zip(part_refs, merged_refs) for ref in pair])
    for y in range(4):
        mine = slice(y * held, (y + 1) * held)
        at = 16 * y
        factor = jnp.exp2(turned[:, at : at + 1] - turned[:, at + 8 : at + 9]) / turned[:, at + 9 : at + 10]
        rows = row_refs[y][:, g].reshape(held, width)
        quant = merged_refs[y][0:held, :]
        error = jnp.where(turned[:, at + 10 : at + 11] > 0.5, quant - rows, 0.0)
        inner = jnp.sum(error * quant, axis=1, keepdims=True) * factor
        scaled = error * factor
        error_ref[mine] = error
        inner_ref[mine] = jnp.broadcast_to(inner, (held, 128))
        high, low = split2(scaled)
        triple_ref[mine] = jnp.concatenate([high, high, low], axis=1)
        for k, value in enumerate((scaled, rows * sharpness)):
            high, low = split2(jnp.transpose(value))
            for part, piece in enumerate((high, low, high)):
                left_ref[:, (3 * k + part) * count + y * held : (3 * k + part) * count + (y + 1) * held] = piece
    if resumed:
        total_ref[...] = before_ref[...]
    else:
        total_ref[...] = jnp.zeros(total_ref.shape, F32)

    @pl.loop(first, first + number)
    def _(b):
        pair = (b - first) // 2
        landed(book_ref, sems, b)
        landed(wide_high, high_sems, b)
        landed(wide_low, low_sems, b)
        ch, cl = split2(book_ref[b])
        right = jnp.concatenate([ch, cl, ch], axis=1)
        inner = inner_ref[...]
        highs, lows = [], []
        for half in range(2):
            align = dot_nt(triple_ref[...], right[half * 256 : (half + 1) * 256])
            for t in range(2):
                at = slice(half * 256 + t * 128, half * 256 + t * 128 + 128)
                w = wide_high[b, :, at].astype(F32) + wide_low[b, :, at].astype(F32)
                sh, sl = split2(w * (align[:, t * 128 : (t + 1) * 128] - inner))
                highs.append(sh)
                lows.append(sl)
        sh = jnp.concatenate(highs, axis=1)
        sl = jnp.concatenate(lows, axis=1)
        wh, wl = wide_high[b], wide_low[b]
        wide_grads[b] = dot_nn(left_ref[...], jnp.concatenate([wh, wh, wl, sh, sh, sl], axis=0))
        total_ref[...] += dot_nn(jnp.concatenate([sh, sl, sh], axis=1), jnp.concatenate([ch, ch, cl], axis=0))

        @pl.when(b % 2 == 0)
        def _():
            pltpu.make_async_copy(wide_grads.at[b], own_ref.at[pair], grads_sems.at[b]).start()

        @pl.when(b % 2 == 1)
        def _():
            pltpu.make_async_copy(wide_grads.at[b], other_ref.at[pair], grads_sems.at[b]).start()

    if final:
        rest = held if joined else 0
        code_row = jnp.concatenate([ref[held + 2 : held + 3, 0:held] for ref in merged_refs], axis=1)
        onehot = (iota((8, count), 0) + 1 == code_row.astype(jnp.int32)).astype(F32)
        coarse = jnp.zeros((8, width), F32)
        for y in range(4):
            mine = slice(y * held, (y + 1) * held)
            pushed = total_ref[mine] * sharpness
            if y == 0:
                pushed = pushed - error_ref[mine]
            pushed_refs[y][rest : rest + held] = pushed
            coarse = coarse - select_rows(onehot[:, mine], pushed)
        if joined:
            for y in range(4):
                pushed_refs[y][0:held] = push0_refs[y][...]
                pushed_refs[y][2 * held : 2 * held + 8] = coarse0_ref[...]
                pushed_refs[y][2 * held + 8 : 2 * held + 16] = coarse
        else:
            coarse_ref[...] = coarse
    else:
        sofar_ref[...] = total_ref[...]
    for b in range(first, first + number):
        out = own_ref if b % 2 == 0 else other_ref
        pltpu.make_async_copy(wide_grads.at[b], out.at[(b - first) // 2], grads_sems.at[b]).wait()


def turn_kernel(own_ref, other_ref, right_ref, left_ref, far_ref, *refs):
    near = (own_ref[0] + other_ref[0]) + (right_ref[...] + left_ref[...])
    refs[-1][0] = jnp.transpose(near + far_ref[...])


def home_kernel(codes_ref, slots_ref, out_ref):
    items, width = out_ref.shape
    group_row, place_row = targets(codes_ref[...], items)
    total = slots_ref.shape[0] * slots_ref.shape[1]
    target = (group_row // 2) * slots_ref.shape[1] + (group_row % 2) * SLOTS + place_row
    target = jnp.transpose(jnp.broadcast_to(target.astype(F32), (items, items)))[:, 0:1].astype(jnp.int32)
    onehot = (target == iota((items, total), 1)).astype(F32)
    out_ref[...] = select_rows(onehot, slots_ref[...].reshape(total, width))


def params(mebibytes=8):
    return pltpu.CompilerParams(vmem_limit_bytes=mebibytes << 20)


def whole(shape, dtype=F32):
    return jax.ShapeDtypeStruct(shape, dtype)


SMEM = pl.BlockSpec(memory_space=pltpu.SMEM)
VMEM = pl.BlockSpec(memory_space=pltpu.VMEM)
ANY = pl.BlockSpec(memory_space=pl.ANY)


def cost(flops, moved, exps=0):
    return pl.CostEstimate(flops=flops, bytes_accessed=moved, transcendentals=exps)


def dmas():
    return pltpu.SemaphoreType.DMA((8,))


def forward(g, rows, blocks):
    width = rows[0].shape[-1]
    count = 512
    return pl.pallas_call(
        functools.partial(forward_kernel, g),
        in_specs=[VMEM] * 4 + [ANY] * 8,
        out_specs=[ANY, ANY] + [VMEM] * 4,
        out_shape=[
            whole((8, count, CHUNK), BF16),
            whole((8, count, CHUNK), BF16),
        ]
        + [whole((HOLD, width))] * 4,
        scratch_shapes=[
            pltpu.VMEM((8, count, CHUNK), F32),
            pltpu.VMEM((count, 3 * width), BF16),
            pltpu.VMEM((8, CHUNK, width), F32),
            pltpu.VMEM((8, CHUNK, width), BF16),
            pltpu.VMEM((8, CHUNK, width), BF16),
            pltpu.VMEM((8, count, CHUNK), BF16),
            pltpu.VMEM((8, count, CHUNK), BF16),
            pltpu.VMEM((count, 128), F32),
            pltpu.VMEM((count, 128), F32),
            pltpu.VMEM((count, width), F32),
            dmas(),
            dmas(),
            dmas(),
        ],
        compiler_params=params(60),
        cost_estimate=cost(12 * count * 8 * CHUNK * width, 12 * count * 8 * CHUNK, count * 8 * CHUNK),
    )(*rows, *blocks)


def backward(g, first, number, rows, part, merged, weights, blocks, before, final, joined=()):
    width = rows[0].shape[-1]
    count = 512
    resumed = before is not None
    out_shape = [whole((number // 2, width, CHUNK))] * 2
    if joined:
        out_shape += [whole((count // 2 + 16, width))] * 4
    elif final:
        out_shape += [whole((count // 4, width))] * 4 + [whole((8, width))]
    else:
        out_shape += [whole((count, width))]
    return pl.pallas_call(
        functools.partial(backward_kernel, g, first, number, resumed, final, bool(joined)),
        in_specs=[VMEM] * 12 + [ANY] * 10 + [VMEM] * (resumed + len(joined)),
        out_specs=[ANY, ANY] + [VMEM] * (len(out_shape) - 2),
        out_shape=out_shape,
        scratch_shapes=[
            pltpu.VMEM((count, 3 * width), BF16),
            pltpu.VMEM((width, 6 * count), BF16),
            pltpu.VMEM((count, 128), F32),
            pltpu.VMEM((count, width), F32),
            pltpu.VMEM((count, width), F32),
            pltpu.VMEM((8, CHUNK, width), F32),
            pltpu.VMEM((8, count, CHUNK), BF16),
            pltpu.VMEM((8, count, CHUNK), BF16),
            pltpu.VMEM((8, width, CHUNK), F32),
            dmas(),
            dmas(),
            dmas(),
            dmas(),
        ],
        compiler_params=params(60),
        cost_estimate=cost(24 * count * number * CHUNK * width, 8 * count * number * CHUNK),
    )(*rows, *part, *merged, *weights, *blocks, *((before,) if resumed else ()), *joined)


def after(value, *others):
    return lax.optimization_barrier((value,) + others)[0]


def step(vectors, item_codes, coarse_book, fine_books):
    items, width = vectors.shape
    shift = lambda a, axis, by: lax.ppermute(a, axis, [(i, (i + by) % 4) for i in range(4)])
    swap = lambda a: lax.ppermute(a, "c", [(0, 1), (1, 0)])
    code_row = item_codes.reshape(1, items)
    z = lax.axis_index("z").astype(jnp.int32).reshape(1)

    def travel(book):
        return [shift(book, "x", by) for by in (1, -1, 2)]

    own = [fine_books[0]]
    near = [travel(own[0])]
    outgoing = pl.pallas_call(
        route_kernel,
        in_specs=[SMEM, VMEM, VMEM, VMEM],
        out_specs=VMEM,
        out_shape=whole((8 * BLOCK, width)),
        compiler_params=params(60),
        name="route",
    )(z, code_row, vectors, coarse_book)
    arrived = lax.all_to_all(outgoing.reshape(4, 2 * BLOCK, width), "z", 0, 0, tiled=True)
    own.append(after(fine_books, arrived)[1])
    near.append(travel(own[1]))
    arrived = arrived.reshape(4, 2, BLOCK, width)
    outward = lambda value: [value] + [shift(value, "y", k) for k in (1, 2, 3)]
    inward = lambda values: [values[0]] + [shift(values[k], "y", -k) for k in (1, 2, 3)]
    rows = outward(arrived[:, :, :SLOTS])

    books, weights, parts = [], [], []
    for g in range(2):
        left, right, far = near[g]
        if g:
            left, right, far, own[g], _ = lax.optimization_barrier((left, right, far, own[g], parts[0][0]))
        blocks = []
        for book in (far, left, right, own[g]):
            blocks += [book, swap(book)]
        high, low, *part = forward(g, rows, blocks)
        books.append(blocks)
        weights.append((high, low))
        parts.append(part)

    def exchange(g, part):
        got = inward(part)
        flat = pl.BlockSpec((HOLD, width), lambda i: (0, 0))
        out = pl.pallas_call(
            merge_kernel,
            grid=(1,),
            in_specs=[flat] * 4 + [pl.BlockSpec((4, 1, BLOCK, width), lambda i: (0, g, 0, 0))],
            out_specs=flat,
            out_shape=whole((HOLD, width)),
            compiler_params=params(),
        )(*got, arrived)
        return outward(out)

    merged = [exchange(0, parts[0]), exchange(1, parts[1])]

    def return_books(g, calls, before):
        pieces = []
        for when, (own, other) in enumerate(calls):
            got = swap(other)
            pieces += [(own, got, i, when) for i in range(own.shape[0])]
        got = []
        for (own, other, i, when), by in zip(pieces, (2, -1, 1)):
            total = own[i] + other[i]
            got.append(shift(total, "x", by))
        own, other, i, _ = pieces[3]
        pair = pl.BlockSpec((1, width, CHUNK), lambda k: (i, 0, 0))
        flat = pl.BlockSpec((width, CHUNK), lambda k: (0, 0))
        return pl.pallas_call(
            turn_kernel,
            grid=(1,),
            in_specs=[pair, pair, flat, flat, flat] + [ANY] * len(before),
            out_specs=pl.BlockSpec((1, CHUNK, width), lambda k: (g, 0, 0)),
            out_shape=whole((2, CHUNK, width)),
            input_output_aliases={5: 0} if before else {},
            compiler_params=params(),
        )(own, other, *got, *before)

    def gradients(g, counts, joined, before):
        common = (rows, parts[g], merged[g], weights[g], books[g])
        calls, first, sofar = [], 0, None
        for number in counts:
            final = first + number == 8
            own, other, *rest = backward(g, first, number, *common, sofar, final, joined if final else ())
            calls.append((own, other))
            first, sofar = first + number, rest[0]
        return return_books(g, calls, before), rest

    fine, joined = gradients(0, (6, 2), (), ())
    fine, push = gradients(1, (8,), tuple(joined), (fine,))

    held = items
    push = inward(push)
    push = (push[0] + push[2]) + (push[1] + push[3])
    coarse = push[2 * held :]
    push = push[: 2 * held].reshape(2, 4, SLOTS, width).transpose(1, 0, 2, 3).reshape(4, 2 * SLOTS, width)
    push = jnp.concatenate([push, jnp.broadcast_to(coarse[None], (4,) + coarse.shape)], axis=1)
    home = lax.all_to_all(push, "z", 0, 0, tiled=True)
    coarse = home[:, 2 * SLOTS :].reshape(-1, width)
    coarse = coarse + swap(coarse)
    others = [shift(coarse, "x", by) for by in (1, 2, 3)]
    coarse = (coarse + others[1]) + (others[0] + others[2])
    item_grad = pl.pallas_call(
        home_kernel,
        in_specs=[VMEM, VMEM],
        out_specs=VMEM,
        out_shape=whole((items, width)),
        compiler_params=params(),
        name="home",
    )(code_row, home)
    return item_grad, fine, coarse


def solution(mesh):
    grid = Mesh(mesh.devices.reshape(4, 4, 4, 2), AXES)
    plane = ("x", "y", "c")
    return jax.shard_map(
        step,
        mesh=grid,
        in_specs=(P(AXES, None), P(AXES), P(), P("z", plane, None)),
        out_specs=(P(AXES, None), P("z", plane, None), P()),
        check_vma=False,
    )
```
